512 devices in a mesh: slab: 128 (over y_lo, z, x), col: 4 (over y_hi, core).
Axes of the slice: x: 4, y: 4 (y_hi: 2, y_lo: 2; y = y_hi * 2 + y_lo), z: 16, core: 2. Of those that a mesh axis runs over, the one named last changes fastest.
Arguments:
- offsets: float32 [3, 256, 8, 4, 128], P(None, 'slab', 'col'), may hold values from 0 to 2
- velocity: float32 [3, 256, 8, 4, 128], P(None, 'slab', 'col'), may hold values from -6 to 6
- occupancy: int32 [256, 8, 4], P('slab', 'col'), may hold values from 32 to 128
Outputs:
- new_offsets: float32 [3, 256, 8, 4, 128], P(None, 'slab', 'col')
- new_velocity: float32 [3, 256, 8, 4, 128], P(None, 'slab', 'col')
- density: float32 [256, 8, 4, 128], P('slab', 'col')
The draws below stay inside these ranges and needn't reach their ends.
All inputs are finite; a program needn't handle non-finite values.
Results may differ from the reference program's by a relative error of at most 0.0001.
Values sent between devices are 32-bit elements; how exact they have to be, the bound alone decides.
No kernel may reach another device: no remote copies, remote signals or barrier semaphores. Data moves between devices by JAX's collectives and lax.ppermute only.
A program may use at most 64 MiB of HBM per device.

```python
import math
import jax
import jax.numpy as jnp
from jax import lax

PPC = 128
STEPS = 2
NX = 256
NY = 8
NZ = 4


def place_ends(result, own_key, least, top_value):
    spot = [jax.random.randint(jax.random.fold_in(own_key, axis), (), 0, length) for axis, length in enumerate(result.shape)]
    widest = result.shape.index(max(result.shape))
    neighbour = spot[:widest] + [(spot[widest] + 1) % result.shape[widest]] + spot[widest + 1:]
    return result.at[tuple(spot)].set(least).at[tuple(neighbour)].set(top_value)


def level_of(own_key, shape, split, least, top_value):
    loudness = 1.0
    for axis_at, parts in split:
        heights = jax.random.uniform(jax.random.fold_in(jax.random.fold_in(own_key, 6), axis_at), (parts,), jnp.float32, least / len(split), top_value / len(split))
        loudness = loudness * jnp.repeat(jnp.exp(heights), shape[axis_at] // parts).reshape((-1,) + (1,) * (len(shape) - 1 - axis_at))
    return loudness


def normal_values(stream_key, extent, spread, bound, pieces=(), kind=jnp.bfloat16):
    result = spread * jax.random.normal(stream_key, extent, jnp.float32)
    if pieces:
        result = result * level_of(stream_key, extent, pieces, -0.22, 0.18)
    return jnp.clip(result, -bound, bound).astype(kind)


def setup_inputs(seed: int = 0) -> dict:
    keys = jax.random.split(jax.random.key(seed), 4)
    offsets = jnp.clip(2.0 * jax.random.uniform(keys[0], (3, NX, NY, NZ, PPC), jnp.float32) ** level_of(keys[0], (3, NX, NY, NZ, PPC), ((1, 128), (2, 4)), -0.2, 0.2), 0.0, 2.0)
    velocity = normal_values(keys[1], (3, NX, NY, NZ, PPC), 1.0, 6.0, ((1, 128), (2, 4)), jnp.float32)
    occupancy = place_ends(jax.random.randint(keys[2], (NX, NY, NZ), PPC // 4, PPC + 1), jax.random.fold_in(keys[2], 1), PPC // 4, PPC).astype(jnp.int32)
    return {"offsets": offsets, "velocity": velocity, "occupancy": occupancy}


kernel_norm = 21.0 / (16.0 * math.pi)
sound_speed = 10.0
tait_coef = sound_speed * sound_speed / 7.0
time_step = 0.02
gravity = 1.0
visc_alpha = 0.2
visc_floor = 0.01
cell_edge = 2.0
plane_steps = [(step_x, step_y) for step_x in (-1, 0, 1) for step_y in (-1, 0, 1)]

def live_slots(count_cells, slot_count):
    slot_rank = jnp.arange(slot_count, dtype=jnp.float32)
    return (slot_rank < count_cells).astype(jnp.float32)

def pair_geometry(target_pos, source_pos, cell_step):
    separation = []
    distance_sq = 0.0
    for axis_num in range(3):
        spacing = target_pos[axis_num][..., :, None] - source_pos[axis_num][..., None, :] - cell_edge * cell_step[axis_num]
        separation.append(spacing)
        distance_sq = distance_sq + spacing * spacing
    return (separation, distance_sq)

def pressure_of(density):
    cubed = density * density * density
    return tait_coef * (cubed * cubed * density - 1.0)

def density_terms(target_pos, source_pos, source_live, cell_step, particle_mass):
    separation, distance_sq = pair_geometry(target_pos, source_pos, cell_step)
    radius = jnp.sqrt(distance_sq)
    inside = jnp.maximum(1.0 - 0.5 * radius, 0.0)
    inside_sq = inside * inside
    weight = kernel_norm * inside_sq * inside_sq * (2.0 * radius + 1.0)
    return particle_mass * lax.optimization_barrier(jnp.sum(weight * source_live[..., None, :], axis=-1))

def force_terms(target, source, cell_step, particle_mass):
    target_pos, target_vel, target_density, target_pressure = target
    source_pos, source_vel, source_density, source_live = source
    source_density = jnp.maximum(source_density, particle_mass * kernel_norm)
    source_pressure = pressure_of(source_density)
    separation, distance_sq = pair_geometry(target_pos, source_pos, cell_step)
    inside = jnp.maximum(1.0 - 0.5 * jnp.sqrt(distance_sq), 0.0)
    slope = -5.0 * kernel_norm * inside * inside * inside
    approach = 0.0
    for axis_num in range(3):
        approach = approach + (target_vel[axis_num][..., :, None] - source_vel[axis_num][..., None, :]) * separation[axis_num]
    closing = jnp.minimum(approach, 0.0) / (distance_sq + visc_floor)
    mean_density = 0.5 * (target_density[..., :, None] + source_density[..., None, :])
    viscous = -visc_alpha * sound_speed * closing / mean_density
    target_ratio = target_pressure / (target_density * target_density)
    source_ratio = source_pressure / (source_density * source_density)
    strength = particle_mass * source_live[..., None, :] * (target_ratio[..., :, None] + source_ratio[..., None, :] + viscous) * slope
    return jnp.stack([-lax.optimization_barrier(jnp.sum(strength * separation[axis_num], axis=-1)) for axis_num in range(3)])

def neighbour_total(term_fn, source_arrays, cells_x, cells_y):
    padded = [jnp.pad(source_arr, ((0, 0), (0, 0), (0, 0), (1, 1), (0, 0))) for source_arr in source_arrays]
    cells_z = source_arrays[0].shape[3]
    slot_count = source_arrays[0].shape[4]
    z_steps = jnp.repeat(jnp.array([-1.0, 0.0, 1.0], dtype=jnp.float32), slot_count)
    running = None
    for step_x, step_y in plane_steps:
        sliced = [jnp.concatenate([source_arr[:, 1 + step_x:1 + step_x + cells_x, 1 + step_y:1 + step_y + cells_y, 1 + step_z:1 + step_z + cells_z] for step_z in (-1, 0, 1)], axis=-1) for source_arr in padded]
        contribution = term_fn(sliced, (step_x, step_y, z_steps))
        running = contribution if running is None else running + contribution
    return running

def density_field(source_pos, source_live, particle_mass):
    cells_x = source_pos.shape[1] - 2
    cells_y = source_pos.shape[2] - 2
    target_pos = source_pos[:, 1:1 + cells_x, 1:1 + cells_y]
    target_live = source_live[0, 1:1 + cells_x, 1:1 + cells_y]

    def term_fn(sliced, cell_step):
        return density_terms(target_pos, sliced[0], sliced[1][0], cell_step, particle_mass)
    summed = neighbour_total(term_fn, [source_pos, source_live], cells_x, cells_y)
    return (summed + (1.0 - target_live) * particle_mass * kernel_norm)[None]

def force_field(source_state, source_density, source_live, particle_mass):
    cells_x = source_state.shape[1] - 2
    cells_y = source_state.shape[2] - 2
    inner = source_state[:, 1:1 + cells_x, 1:1 + cells_y]
    target_density = jnp.maximum(source_density[0, 1:1 + cells_x, 1:1 + cells_y], particle_mass * kernel_norm)
    target = (inner[0:3], inner[3:6], target_density, pressure_of(target_density))

    def term_fn(sliced, cell_step):
        return force_terms(target, (sliced[0][0:3], sliced[0][3:6], sliced[1][0], sliced[2][0]), cell_step, particle_mass)
    return neighbour_total(term_fn, [source_state, source_density, source_live], cells_x, cells_y)

def advance(particle_state, acceleration, own_live):
    gravity_pull = jnp.array([0.0, 0.0, gravity], dtype=jnp.float32)[:, None, None, None, None]
    new_vel = particle_state[3:6] + time_step * (acceleration - gravity_pull)
    new_pos = particle_state[0:3] + time_step * new_vel
    updated = jnp.concatenate([new_pos, new_vel], axis=0)
    return own_live * updated + (1.0 - own_live) * particle_state

def reference(offsets, velocity, occupancy):
    slot_count = offsets.shape[-1]
    particle_mass = 8.0 / slot_count
    particle_state = jnp.concatenate([offsets, velocity], axis=0)
    count_cells = occupancy.astype(jnp.float32)[None, :, :, :, None]
    own_live = live_slots(count_cells, slot_count)
    margin = ((0, 0), (1, 1), (1, 1), (0, 0), (0, 0))
    padded_live = jnp.pad(own_live, margin)
    columns = jnp.arange(offsets.shape[1], dtype=jnp.int32)
    density = None
    for section_num in range(STEPS):
        padded_state = jnp.pad(particle_state, margin)

        def column_density(column):
            source_pos = lax.dynamic_slice_in_dim(padded_state[0:3], column, 3, 1)
            source_live = lax.dynamic_slice_in_dim(padded_live, column, 3, 1)
            return density_field(source_pos, source_live, particle_mass)[:, 0]
        density = jnp.moveaxis(lax.map(column_density, columns), 0, 1)
        padded_density = jnp.pad(density, margin)

        def column_force(column):
            source_state = lax.dynamic_slice_in_dim(padded_state, column, 3, 1)
            source_density = lax.dynamic_slice_in_dim(padded_density, column, 3, 1)
            source_live = lax.dynamic_slice_in_dim(padded_live, column, 3, 1)
            return force_field(source_state, source_density, source_live, particle_mass)[:, 0]
        acceleration = jnp.moveaxis(lax.map(column_force, columns), 0, 1)
        particle_state = advance(particle_state, acceleration, own_live)
    return (particle_state[0:3], particle_state[3:6], density[0])
```

```python
import functools
import math

import jax
import jax.numpy as jnp
from jax import lax
from jax.experimental import pallas as pl
from jax.experimental.pallas import tpu as pltpu
from jax.sharding import PartitionSpec as P

STEPS = 2
SLOTS = 128
MASS = 8.0 / SLOTS
KERNEL_NORM = 21.0 / (16.0 * math.pi)
TAIT = 10.0 * 10.0 / 7.0
TIME_STEP = 0.02
GRAVITY = 1.0
FAR = 1000.0
TINY = 1e-30

PARTS_J = (0, 0, 1, 1, 0, 2)
PARTS_I = (0, 1, 0, 1, 2, 0)
ROW_X = 0
ROW_NJ = 18
ROW_ONE = 21
ROW_V = 24
ROW_WJ = 42
ROW_RHO = 45
ROW_P = 48
DEPTH = 128


def split3(value):
    high = value.astype(jnp.bfloat16).astype(jnp.float32)
    rest = value - high
    middle = rest.astype(jnp.bfloat16).astype(jnp.float32)
    return (high, middle, rest - middle)


def cell_z(rows):
    return lax.broadcasted_iota(jnp.int32, (rows, SLOTS), 0).astype(jnp.float32)


def dot(lhs, rhs):
    return jnp.dot(lhs, rhs, preferred_element_type=jnp.float32)


def fold(tile):
    return jnp.sum(tile.reshape(tile.shape[0] // 8, 8, tile.shape[1]), axis=0)


def column_of(refs, comp, ix, iy):
    own, left, right, down, up = refs
    if iy == 0:
        return down[comp, ix]
    if iy == 3:
        return up[comp, ix]
    if ix < 2:
        return left[comp, ix, iy - 1]
    if ix < 4:
        return own[comp, ix - 2, iy - 1]
    return right[comp, ix - 4, iy - 1]


def centred(refs, ix, iy):
    shifts = (ix - 3.0, iy - 2.0, None)
    places = []
    for axis in range(3):
        half = 0.5 * column_of(refs, axis, ix, iy)
        shift = shifts[axis] if axis < 2 else cell_z(half.shape[0]) - 0.5 * half.shape[0]
        places.append(half + shift)
    return places


def source_rows(refs, ix, iy, with_velocity):
    live = column_of(refs, 6, ix, iy) > 0.5
    places = [jnp.where(live, place, FAR) for place in centred(refs, ix, iy)]
    rows = {}
    for axis in range(3):
        parts = split3(places[axis])
        for at, part in enumerate(PARTS_J):
            rows[ROW_X + 6 * axis + at] = parts[part]
    norm = places[0] * places[0] + places[1] * places[1] + places[2] * places[2]
    for at, part in enumerate(split3(norm)):
        rows[ROW_NJ + at] = part
        rows[ROW_ONE + at] = jnp.ones_like(part)
    if with_velocity:
        speeds = [column_of(refs, 3 + axis, ix, iy) for axis in range(3)]
        along = 0.0
        for axis in range(3):
            parts = split3(speeds[axis])
            for at, part in enumerate(PARTS_J):
                rows[ROW_V + 6 * axis + at] = parts[part]
            along = along + speeds[axis] * places[axis]
        for at, part in enumerate(split3(along)):
            rows[ROW_WJ + at] = part
    return rows


def put_rows(table, column, rows):
    for row, value in rows.items():
        table[column, :, row, :] = value


def turn_tables(table, turned, columns, cells_z):
    def body(step, carry):
        column, z = step // cells_z, step % cells_z
        turned[column, z] = jnp.transpose(table[column, z]).astype(jnp.bfloat16)
        return carry

    lax.fori_loop(0, columns * cells_z, body, 0)


def density_kernel(own, left, right, down, up, rho_ref, table, turned, weights):
    refs = (own, left, right, down, up)
    cells_z = own.shape[3]
    table[...] = jnp.zeros_like(table)
    weights[...] = jnp.zeros_like(weights)
    for ix in range(6):
        for iy in range(4):
            put_rows(table, ix * 4 + iy, source_rows(refs, ix, iy, False))
    turn_tables(table, turned, 24, cells_z)
    for tx in range(4):
        for ty in range(2):
            places = centred(refs, tx + 1, ty + 1)
            rows = {}
            for axis in range(3):
                parts = split3(-2.0 * places[axis])
                for at, part in enumerate(PARTS_I):
                    rows[ROW_X + 6 * axis + at] = parts[part]
            norm = places[0] * places[0] + places[1] * places[1] + places[2] * places[2]
            for at, part in enumerate(split3(norm)):
                rows[ROW_NJ + at] = jnp.ones_like(part)
                rows[ROW_ONE + at] = part
            put_rows(weights, tx * 2 + ty, rows)

    def target(step, carry):
        tx, ty = step // 2, step % 2
        rhs = [
            jnp.concatenate(
                [weights[step, 2 * pair].astype(jnp.bfloat16), weights[step, 2 * pair + 1].astype(jnp.bfloat16)], axis=1
            )
            for pair in range(cells_z // 2)
        ]

        def source(dx, sums):
            sums = list(sums)
            for dy in range(3):
                column = (tx + dx) * 4 + ty + dy
                for pair in range(cells_z // 2):
                    for z in range(max(0, 2 * pair - 1), min(cells_z, 2 * pair + 3)):
                        gap = dot(turned[column, z], rhs[pair])
                        for half in range(2):
                            zt = 2 * pair + half
                            if abs(zt - z) > 1:
                                continue
                            near = jnp.maximum(gap[:, half * SLOTS : (half + 1) * SLOTS], TINY)
                            inside = jnp.maximum(1.0 - near * lax.rsqrt(near), 0.0)
                            square = inside * inside
                            fourth = square * square
                            sums[2 * zt] = sums[2 * zt] + fold(fourth)
                            sums[2 * zt + 1] = sums[2 * zt + 1] + fold(fourth * inside)
            return tuple(sums)

        zero = jnp.zeros((8, SLOTS), jnp.float32)
        sums = lax.fori_loop(0, 3, source, (zero,) * (2 * cells_z))
        for zt in range(cells_z):
            total = 5.0 * sums[2 * zt] - 4.0 * sums[2 * zt + 1]
            rho_ref[tx, ty, pl.ds(zt, 1), :] = (MASS * KERNEL_NORM) * jnp.sum(total, axis=0, keepdims=True)
        return carry

    lax.fori_loop(0, 8, target, 0)
    for ix in range(2):
        for iy in range(2):
            rho_ref[ix + 1, iy] = rho_ref[ix + 1, iy] + (1.0 - own[6, ix, iy]) * (MASS * KERNEL_NORM)


def pressure_ratio(density):
    cubed = density * density * density
    return TAIT * (cubed * cubed * density - 1.0) / (density * density)


def force_kernel(own, left, right, down, up, rho, rho_down, rho_up, out_ref, table, turned, weights, spread, rows_i):
    refs = (own, left, right, down, up)
    cells_z = own.shape[3]
    table[...] = jnp.zeros_like(table)
    weights[...] = jnp.zeros_like(weights)
    for ix in range(4):
        for iy in range(4):
            rows = source_rows(refs, ix + 1, iy, True)
            density = rho_down[ix] if iy == 0 else rho_up[ix] if iy == 3 else rho[ix, iy - 1]
            density = jnp.maximum(density, MASS * KERNEL_NORM)
            for at, part in enumerate(split3(density)):
                rows[ROW_RHO + at] = part
            for at, part in enumerate(split3(pressure_ratio(density))):
                rows[ROW_P + at] = part
            put_rows(table, ix * 4 + iy, rows)
    turn_tables(table, turned, 16, cells_z)

    at_row = lax.broadcasted_iota(jnp.int32, (DEPTH, SLOTS), 0)
    picks = []
    for rows in (
        tuple(range(ROW_RHO, ROW_RHO + 3)),
        tuple(range(ROW_P, ROW_P + 3)),
        (ROW_X, ROW_X + 2, ROW_X + 5),
        (ROW_X + 6, ROW_X + 8, ROW_X + 11),
        (ROW_X + 12, ROW_X + 14, ROW_X + 17),
    ):
        chosen = (at_row == rows[0]) | (at_row == rows[1]) | (at_row == rows[2])
        picks.append(jnp.where(chosen, 1.0, 0.0).astype(jnp.bfloat16))

    def spread_cell(step, carry):
        column, z = step // cells_z, step % cells_z
        for at, pick in enumerate(picks):
            spread[column, z, at] = dot(turned[column, z], pick)
        return carry

    lax.fori_loop(0, 16 * cells_z, spread_cell, 0)

    for tx in range(2):
        for ty in range(2):
            places = centred(refs, tx + 2, ty + 1)
            speeds = [column_of(refs, 3 + axis, tx + 2, ty + 1) for axis in range(3)]
            gap_rows, near_rows = {}, {}
            norm, along = 0.0, 0.0
            for axis in range(3):
                gap_parts = split3(-2.0 * places[axis])
                place_parts = split3(2.0 * places[axis])
                speed_parts = split3(2.0 * speeds[axis])
                for at, part in enumerate(PARTS_I):
                    gap_rows[ROW_X + 6 * axis + at] = gap_parts[part]
                    near_rows[ROW_X + 6 * axis + at] = speed_parts[part]
                    near_rows[ROW_V + 6 * axis + at] = place_parts[part]
                norm = norm + places[axis] * places[axis]
                along = along + places[axis] * speeds[axis]
            for at, (part, other) in enumerate(zip(split3(norm), split3(-2.0 * along))):
                gap_rows[ROW_NJ + at] = jnp.ones_like(part)
                gap_rows[ROW_ONE + at] = part
                near_rows[ROW_WJ + at] = jnp.full_like(part, -2.0)
                near_rows[ROW_ONE + at] = other
            put_rows(weights.at[0], tx * 2 + ty, gap_rows)
            put_rows(weights.at[1], tx * 2 + ty, near_rows)
            density = jnp.maximum(rho[tx + 1, ty], MASS * KERNEL_NORM)
            rows_i[tx * 2 + ty, 0] = density
            rows_i[tx * 2 + ty, 1] = pressure_ratio(density)
            for axis in range(3):
                rows_i[tx * 2 + ty, 2 + axis] = places[axis]

    def target(step, carry):
        tx, ty = step // 2, step % 2
        rhs = [
            jnp.concatenate([weights[0, step, z].astype(jnp.bfloat16), weights[1, step, z].astype(jnp.bfloat16)], axis=1)
            for z in range(cells_z)
        ]
        rho_i = [rows_i[step, 0, pl.ds(z, 1), :] for z in range(cells_z)]
        ratio_i = [rows_i[step, 1, pl.ds(z, 1), :] for z in range(cells_z)]

        def source(dx, sums):
            sums = list(sums)
            for dy in range(3):
                column = (tx + dx) * 4 + ty + dy
                for zt in range(cells_z):
                    for z in range(max(0, zt - 1), min(cells_z, zt + 2)):
                        both = dot(turned[column, z], rhs[zt])
                        near = jnp.maximum(both[:, :SLOTS], TINY)
                        inside = jnp.maximum(1.0 - near * lax.rsqrt(near), 0.0)
                        closing = jnp.maximum(both[:, SLOTS:], 0.0)
                        below = (near + 0.0025) * (spread[column, z, 0] + rho_i[zt])
                        strength = (spread[column, z, 1] + ratio_i[zt]) + closing / below
                        strength = strength * (inside * inside * inside)
                        sums[4 * zt] = sums[4 * zt] + fold(strength)
                        for axis in range(3):
                            sums[4 * zt + 1 + axis] = sums[4 * zt + 1 + axis] + fold(strength * spread[column, z, 2 + axis])
            return tuple(sums)

        zero = jnp.zeros((8, SLOTS), jnp.float32)
        sums = lax.fori_loop(0, 3, source, (zero,) * (4 * cells_z))
        for zt in range(cells_z):
            row = pl.ds(zt, 1)
            whole = jnp.sum(sums[4 * zt], axis=0, keepdims=True)
            live = own[6, tx, ty, row, :] > 0.5
            for axis in range(3):
                part = jnp.sum(sums[4 * zt + 1 + axis], axis=0, keepdims=True)
                pull = (10.0 * KERNEL_NORM * MASS) * (rows_i[step, 2 + axis, row, :] * whole - part)
                if axis == 2:
                    pull = pull - GRAVITY
                old_place = own[axis, tx, ty, row, :]
                old_speed = own[3 + axis, tx, ty, row, :]
                speed = old_speed + TIME_STEP * pull
                out_ref[axis, tx, ty, row, :] = jnp.where(live, old_place + TIME_STEP * speed, old_place)
                out_ref[3 + axis, tx, ty, row, :] = jnp.where(live, speed, old_speed)
            out_ref[6, tx, ty, row, :] = own[6, tx, ty, row, :]
        return carry

    lax.fori_loop(0, 4, target, 0)


VMEM_SPEC = pl.BlockSpec(memory_space=pltpu.VMEM)


def densities(state, left, right, down, up):
    cells_z = state.shape[3]
    return pl.pallas_call(
        density_kernel,
        name="density",
        out_shape=jax.ShapeDtypeStruct((4, 2, cells_z, SLOTS), jnp.float32),
        in_specs=[VMEM_SPEC] * 5,
        out_specs=VMEM_SPEC,
        scratch_shapes=[
            pltpu.VMEM((24, cells_z, DEPTH, SLOTS), jnp.float32),
            pltpu.VMEM((24, cells_z, SLOTS, DEPTH), jnp.bfloat16),
            pltpu.VMEM((8, cells_z, DEPTH, SLOTS), jnp.float32),
        ],
        compiler_params=pltpu.CompilerParams(vmem_limit_bytes=48 << 20),
    )(state, left, right, down, up)


def moved(state, left, right, down, up, rho, rho_down, rho_up):
    cells_z = state.shape[3]
    return pl.pallas_call(
        force_kernel,
        name="force",
        out_shape=jax.ShapeDtypeStruct(state.shape, jnp.float32),
        in_specs=[VMEM_SPEC] * 8,
        out_specs=VMEM_SPEC,
        scratch_shapes=[
            pltpu.VMEM((16, cells_z, DEPTH, SLOTS), jnp.float32),
            pltpu.VMEM((16, cells_z, SLOTS, DEPTH), jnp.bfloat16),
            pltpu.VMEM((2, 4, cells_z, DEPTH, SLOTS), jnp.float32),
            pltpu.VMEM((16, cells_z, 5, SLOTS, SLOTS), jnp.float32),
            pltpu.VMEM((4, 5, cells_z, SLOTS), jnp.float32),
        ],
        compiler_params=pltpu.CompilerParams(vmem_limit_bytes=56 << 20),
    )(state, left, right, down, up, rho, rho_down, rho_up)


def from_below(value, axis):
    count = lax.axis_size(axis)
    return lax.ppermute(value, axis, [(i, i + 1) for i in range(count - 1)])


def from_above(value, axis):
    count = lax.axis_size(axis)
    return lax.ppermute(value, axis, [(i + 1, i) for i in range(count - 1)])


def per_device(offsets, velocity, occupancy):
    slot_rank = jnp.arange(SLOTS, dtype=jnp.int32)
    live = (slot_rank < occupancy[..., None]).astype(jnp.float32)
    state = jnp.concatenate([offsets, velocity, live[None]], axis=0)
    rho = None
    for _ in range(STEPS):
        left, right = from_below(state, "slab"), from_above(state, "slab")
        edge = lambda y: jnp.concatenate([left[:, :, y], state[:, :, y], right[:, :, y]], axis=1)
        down, up = from_below(edge(1), "col"), from_above(edge(0), "col")
        rho = densities(state, left, right, down, up)
        rho_down, rho_up = from_below(rho[:, 1], "col"), from_above(rho[:, 0], "col")
        state = moved(state, left, right, down, up, rho, rho_down, rho_up)
    return (state[0:3], state[3:6], rho[1:3])


def solution(mesh):
    placed = P(None, "slab", "col", None, None)
    return jax.shard_map(
        per_device,
        mesh=mesh,
        in_specs=(placed, placed, P("slab", "col", None)),
        out_specs=(placed, placed, P("slab", "col", None, None)),
        check_vma=False,
    )
```

```python
import functools
import math

import jax
import jax.numpy as jnp
from jax import lax
from jax.experimental import pallas as pl
from jax.experimental.pallas import tpu as pltpu
from jax.sharding import PartitionSpec as P

STEPS = 2
SLOTS = 128
MASS = 8.0 / SLOTS
KERNEL_NORM = 21.0 / (16.0 * math.pi)
TAIT = 10.0 * 10.0 / 7.0
TIME_STEP = 0.02
GRAVITY = 1.0
FAR = 1000.0
TINY = 1e-30

PARTS_J = (0, 0, 1, 1, 0, 2)
PARTS_I = (0, 1, 0, 1, 2, 0)
ROW_X = 0
ROW_NJ = 18
ROW_ONE = 21
ROW_V = 24
ROW_WJ = 42
ROW_RHO = 45
ROW_P = 48
SHORT = 32
LONG = 64
DEPTH = 128
SUM_ROWS = ((ROW_X, ROW_X + 2, ROW_X + 5), (ROW_X + 6, ROW_X + 8, ROW_X + 11), (ROW_X + 12, ROW_X + 14, ROW_X + 17))


def split3(value):
    high = value.astype(jnp.bfloat16).astype(jnp.float32)
    rest = value - high
    middle = rest.astype(jnp.bfloat16).astype(jnp.float32)
    return (high, middle, rest - middle)


def dot(lhs, rhs):
    return jnp.dot(lhs, rhs, preferred_element_type=jnp.float32)


def fold(tile):
    return jnp.sum(tile.reshape(tile.shape[0] // 8, 8, tile.shape[1]), axis=0)


def parities():
    return lax.axis_index("slab") % 2 == 0, lax.axis_index("col") % 2 == 0


def column_of(refs, comp, ix, iy):
    own, slab_a, slab_b, col_a, col_b = refs
    slab_even, col_even = parities()
    if iy in (0, 3):
        near, other = (col_b, col_a) if iy == 0 else (col_a, col_b)
        rows = lambda at: jnp.where(col_even, near[comp, at], other[comp, at])
        if 2 <= ix < 4:
            return rows(ix)
        at_a, at_b = ix % 2, 4 + ix % 2
        first, second = (at_b, at_a) if ix < 2 else (at_a, at_b)
        return jnp.where(slab_even, rows(first), rows(second))
    if 2 <= ix < 4:
        return own[comp, ix - 2, iy - 1]
    first, second = (slab_b, slab_a) if ix < 2 else (slab_a, slab_b)
    return jnp.where(slab_even, first[comp, ix % 2, iy - 1], second[comp, ix % 2, iy - 1])


def centred(refs, ix, iy):
    places = []
    for axis in range(3):
        half = 0.5 * column_of(refs, axis, ix, iy)
        if axis == 2:
            shift = lax.broadcasted_iota(jnp.int32, half.shape, 0).astype(jnp.float32) - 0.5 * half.shape[0]
        else:
            shift = (ix - 3.0, iy - 2.0)[axis]
        places.append(half + shift)
    return places


def source_rows(refs, ix, iy, with_velocity):
    live = column_of(refs, 6, ix, iy) > 0.5
    places = [jnp.where(live, place, FAR) for place in centred(refs, ix, iy)]
    rows = {}
    for axis in range(3):
        parts = split3(places[axis])
        for at, part in enumerate(PARTS_J):
            rows[ROW_X + 6 * axis + at] = parts[part]
    norm = places[0] * places[0] + places[1] * places[1] + places[2] * places[2]
    for at, part in enumerate(split3(norm)):
        rows[ROW_NJ + at] = part
        rows[ROW_ONE + at] = jnp.ones_like(part)
    if with_velocity:
        speeds = [column_of(refs, 3 + axis, ix, iy) for axis in range(3)]
        along = 0.0
        for axis in range(3):
            parts = split3(speeds[axis])
            for at, part in enumerate(PARTS_J):
                rows[ROW_V + 6 * axis + at] = parts[part]
            along = along + speeds[axis] * places[axis]
        for at, part in enumerate(split3(along)):
            rows[ROW_WJ + at] = part
    return rows


def put_rows(table, column, rows, depth):
    blank = jnp.zeros((table.shape[1], SLOTS), jnp.float32)
    for row in range(depth):
        table[column, :, row, :] = rows.get(row, blank)


def turned_cell(table, column, z):
    rows = table[column, z]
    flat = jnp.transpose(rows)
    return jnp.concatenate([flat, jnp.zeros((SLOTS, DEPTH - rows.shape[0]), jnp.float32)], axis=1).astype(jnp.bfloat16)


def deep(rows):
    return jnp.concatenate([rows, jnp.zeros((DEPTH - rows.shape[0], SLOTS), jnp.float32)], axis=0).astype(jnp.bfloat16)


def density_kernel(own, slab_a, slab_b, col_a, col_b, rho_ref, send_a, send_b, table, turned, weights):
    refs = (own, slab_a, slab_b, col_a, col_b)
    cells_z = own.shape[3]
    for ix in range(6):
        for iy in range(4):
            put_rows(table, ix * 4 + iy, source_rows(refs, ix, iy, False), SHORT)

    def turn(column, carry):
        for z in range(cells_z):
            turned[column, z] = turned_cell(table, column, z)
        return carry

    lax.fori_loop(0, 24, turn, 0)
    for tx in range(4):
        for ty in range(2):
            places = centred(refs, tx + 1, ty + 1)
            rows = {}
            for axis in range(3):
                parts = split3(-2.0 * places[axis])
                for at, part in enumerate(PARTS_I):
                    rows[ROW_X + 6 * axis + at] = parts[part]
            norm = places[0] * places[0] + places[1] * places[1] + places[2] * places[2]
            for at, part in enumerate(split3(norm)):
                rows[ROW_NJ + at] = jnp.ones_like(part)
                rows[ROW_ONE + at] = part
            put_rows(weights, tx * 2 + ty, rows, SHORT)

    def target(step, carry):
        tx, ty = step // 2, step % 2
        rhs = [
            jnp.concatenate([deep(weights[step, 2 * pair]), deep(weights[step, 2 * pair + 1])], axis=1)
            for pair in range(cells_z // 2)
        ]

        def source(dx, sums):
            sums = list(sums)
            for dy in range(3):
                column = (tx + dx) * 4 + ty + dy
                for pair in range(cells_z // 2):
                    for z in range(max(0, 2 * pair - 1), min(cells_z, 2 * pair + 3)):
                        gap = dot(turned[column, z], rhs[pair])
                        for half in range(2):
                            zt = 2 * pair + half
                            if abs(zt - z) > 1:
                                continue
                            near = jnp.maximum(gap[:, half * SLOTS : (half + 1) * SLOTS], TINY)
                            inside = jnp.maximum(1.0 - near * lax.rsqrt(near), 0.0)
                            square = inside * inside
                            fourth = square * square
                            sums[2 * zt] = sums[2 * zt] + fold(fourth)
                            sums[2 * zt + 1] = sums[2 * zt + 1] + fold(fourth * inside)
            return tuple(sums)

        zero = jnp.zeros((8, SLOTS), jnp.float32)
        sums = lax.fori_loop(0, 3, source, (zero,) * (2 * cells_z))
        for zt in range(cells_z):
            total = 5.0 * sums[2 * zt] - 4.0 * sums[2 * zt + 1]
            rho_ref[tx, ty, pl.ds(zt, 1), :] = (MASS * KERNEL_NORM) * jnp.sum(total, axis=0, keepdims=True)
        return carry

    lax.fori_loop(0, 8, target, 0)
    for ix in range(2):
        for iy in range(2):
            rho_ref[ix + 1, iy] = rho_ref[ix + 1, iy] + (1.0 - own[6, ix, iy]) * (MASS * KERNEL_NORM)
    col_even = parities()[1]
    for ix in range(4):
        low, high = rho_ref[ix, 0], rho_ref[ix, 1]
        send_a[ix] = jnp.where(col_even, high, low)
        send_b[ix] = jnp.where(col_even, low, high)


def pressure_ratio(density):
    cubed = density * density * density
    return TAIT * (cubed * cubed * density - 1.0) / (density * density)


def force_kernel(
    last, own, slab_a, slab_b, col_a, col_b, rho, rho_a, rho_b, place_ref, speed_ref, table, turned, weights, spread, rows_i
):
    refs = (own, slab_a, slab_b, col_a, col_b)
    cells_z = own.shape[3]
    col_even = parities()[1]
    for ix in range(4):
        for iy in range(4):
            rows = source_rows(refs, ix + 1, iy, True)
            if iy == 0:
                density = jnp.where(col_even, rho_b[ix], rho_a[ix])
            elif iy == 3:
                density = jnp.where(col_even, rho_a[ix], rho_b[ix])
            else:
                density = rho[ix, iy - 1]
            density = jnp.maximum(density, MASS * KERNEL_NORM)
            for at, part in enumerate(split3(density)):
                rows[ROW_RHO + at] = part
            for at, part in enumerate(split3(pressure_ratio(density))):
                rows[ROW_P + at] = part
            put_rows(table, ix * 4 + iy, rows, LONG)

    at_row = lax.broadcasted_iota(jnp.int32, (DEPTH, SLOTS), 0)
    picks = []
    for rows in SUM_ROWS + (tuple(range(ROW_RHO, ROW_RHO + 3)), tuple(range(ROW_P, ROW_P + 3))):
        chosen = (at_row == rows[0]) | (at_row == rows[1]) | (at_row == rows[2])
        picks.append(jnp.where(chosen, 1.0, 0.0).astype(jnp.bfloat16))

    def turn(column, carry):
        for z in range(cells_z):
            flat = turned_cell(table, column, z)
            turned[column, z] = flat
            for at, pick in enumerate(picks):
                spread[column, z, at] = dot(flat, pick)
        return carry

    lax.fori_loop(0, 16, turn, 0)

    for tx in range(2):
        for ty in range(2):
            places = centred(refs, tx + 2, ty + 1)
            speeds = [column_of(refs, 3 + axis, tx + 2, ty + 1) for axis in range(3)]
            gap_rows, near_rows = {}, {}
            norm, along = 0.0, 0.0
            for axis in range(3):
                gap_parts = split3(-2.0 * places[axis])
                place_parts = split3(2.0 * places[axis])
                speed_parts = split3(2.0 * speeds[axis])
                for at, part in enumerate(PARTS_I):
                    gap_rows[ROW_X + 6 * axis + at] = gap_parts[part]
                    near_rows[ROW_X + 6 * axis + at] = speed_parts[part]
                    near_rows[ROW_V + 6 * axis + at] = place_parts[part]
                norm = norm + places[axis] * places[axis]
                along = along + places[axis] * speeds[axis]
            for at, (part, other) in enumerate(zip(split3(norm), split3(-2.0 * along))):
                gap_rows[ROW_NJ + at] = jnp.ones_like(part)
                gap_rows[ROW_ONE + at] = part
                near_rows[ROW_WJ + at] = jnp.full_like(part, -2.0)
                near_rows[ROW_ONE + at] = other
            put_rows(weights.at[0], tx * 2 + ty, gap_rows, LONG)
            put_rows(weights.at[1], tx * 2 + ty, near_rows, LONG)
            density = jnp.maximum(rho[tx + 1, ty], MASS * KERNEL_NORM)
            rows_i[tx * 2 + ty, 0] = density
            rows_i[tx * 2 + ty, 1] = pressure_ratio(density)
            for axis in range(3):
                rows_i[tx * 2 + ty, 2 + axis] = places[axis]

    def target(step, carry):
        tx, ty = step // 2, step % 2
        rhs = [jnp.concatenate([deep(weights[0, step, z]), deep(weights[1, step, z])], axis=1) for z in range(cells_z)]
        rho_i = [rows_i[step, 0, pl.ds(z, 1), :] for z in range(cells_z)]
        ratio_i = [rows_i[step, 1, pl.ds(z, 1), :] for z in range(cells_z)]

        def source(dx, sums):
            sums = list(sums)
            for dy in range(3):
                column = (tx + dx) * 4 + ty + dy
                for zt in range(cells_z):
                    for z in range(max(0, zt - 1), min(cells_z, zt + 2)):
                        both = dot(turned[column, z], rhs[zt])
                        near = jnp.maximum(both[:, :SLOTS], TINY)
                        inside = jnp.maximum(1.0 - near * lax.rsqrt(near), 0.0)
                        closing = jnp.maximum(both[:, SLOTS:], 0.0)
                        below = (near + 0.0025) * (spread[column, z, 3] + rho_i[zt])
                        strength = (spread[column, z, 4] + ratio_i[zt]) + closing / below
                        strength = strength * (inside * inside * inside)
                        for axis in range(3):
                            sums[4 * zt + axis] = sums[4 * zt + axis] + fold(strength * spread[column, z, axis])
                        sums[4 * zt + 3] = sums[4 * zt + 3] + fold(strength)
            return tuple(sums)

        zero = jnp.zeros((8, SLOTS), jnp.float32)
        sums = lax.fori_loop(0, 3, source, (zero,) * (4 * cells_z))
        for zt in range(cells_z):
            row = pl.ds(zt, 1)
            *parts, whole = [jnp.sum(total, axis=0, keepdims=True) for total in sums[4 * zt : 4 * zt + 4]]
            live = own[6, tx, ty, row, :] > 0.5
            for axis in range(3):
                pull = (10.0 * KERNEL_NORM * MASS) * (rows_i[step, 2 + axis, row, :] * whole - parts[axis])
                if axis == 2:
                    pull = pull - GRAVITY
                old_place = own[axis, tx, ty, row, :]
                old_speed = own[3 + axis, tx, ty, row, :]
                speed = old_speed + TIME_STEP * pull
                place_ref[axis, tx, ty, row, :] = jnp.where(live, old_place + TIME_STEP * speed, old_place)
                speed_at = axis if last else 3 + axis
                speed_ref[speed_at, tx, ty, row, :] = jnp.where(live, speed, old_speed)
            if not last:
                place_ref[6, tx, ty, row, :] = own[6, tx, ty, row, :]
        return carry

    lax.fori_loop(0, 4, target, 0)


def middle_force_kernel(own, a, b, c, d, rho, rho_a, rho_b, out_ref, *scratch):
    force_kernel(False, own, a, b, c, d, rho, rho_a, rho_b, out_ref, out_ref, *scratch)


VMEM_SPEC = pl.BlockSpec(memory_space=pltpu.VMEM)


def shaped(*shape):
    return jax.ShapeDtypeStruct(shape, jnp.float32)


def densities(state, slab_a, slab_b, col_a, col_b):
    cells_z = state.shape[3]
    return pl.pallas_call(
        density_kernel,
        name="density",
        out_shape=(shaped(4, 2, cells_z, SLOTS), shaped(4, cells_z, SLOTS), shaped(4, cells_z, SLOTS)),
        in_specs=[VMEM_SPEC] * 5,
        out_specs=(VMEM_SPEC,) * 3,
        scratch_shapes=[
            pltpu.VMEM((24, cells_z, SHORT, SLOTS), jnp.float32),
            pltpu.VMEM((24, cells_z, SLOTS, DEPTH), jnp.bfloat16),
            pltpu.VMEM((8, cells_z, SHORT, SLOTS), jnp.float32),
        ],
        compiler_params=pltpu.CompilerParams(vmem_limit_bytes=32 << 20),
    )(state, slab_a, slab_b, col_a, col_b)


def moved(last, state, slab_a, slab_b, col_a, col_b, rho, rho_a, rho_b):
    cells_z = state.shape[3]
    block = state.shape[1:]
    return pl.pallas_call(
        functools.partial(force_kernel, True) if last else middle_force_kernel,
        name="force",
        out_shape=(shaped(3, *block), shaped(3, *block)) if last else shaped(7, *block),
        in_specs=[VMEM_SPEC] * 8,
        out_specs=(VMEM_SPEC, VMEM_SPEC) if last else VMEM_SPEC,
        scratch_shapes=[
            pltpu.VMEM((16, cells_z, LONG, SLOTS), jnp.float32),
            pltpu.VMEM((16, cells_z, SLOTS, DEPTH), jnp.bfloat16),
            pltpu.VMEM((2, 4, cells_z, LONG, SLOTS), jnp.float32),
            pltpu.VMEM((16, cells_z, 5, SLOTS, SLOTS), jnp.float32),
            pltpu.VMEM((4, 5, cells_z, SLOTS), jnp.float32),
        ],
        compiler_params=pltpu.CompilerParams(vmem_limit_bytes=40 << 20),
    )(state, slab_a, slab_b, col_a, col_b, rho, rho_a, rho_b)


def swap_even(value, axis):
    return lax.ppermute(value, axis, [(i, i ^ 1) for i in range(lax.axis_size(axis))])


def swap_odd(value, axis):
    count = lax.axis_size(axis)
    return lax.ppermute(value, axis, [(i, i - 1 if i % 2 == 0 else i + 1) for i in range(1, count - 1)])


def per_device(offsets, velocity, occupancy):
    slot_rank = jnp.arange(SLOTS, dtype=jnp.int32)
    live = (slot_rank < occupancy[..., None]).astype(jnp.float32)
    state = jnp.concatenate([offsets, velocity, live[None]], axis=0)
    col_odd = lax.axis_index("col") % 2
    for section in range(STEPS):
        slab_b, slab_a = swap_odd(state, "slab"), swap_even(state, "slab")
        edges = [
            jnp.concatenate([lax.dynamic_index_in_dim(part, y, 2, keepdims=False) for part in (slab_a, state, slab_b)], axis=1)
            for y in (col_odd, 1 - col_odd)
        ]
        col_b, col_a = swap_odd(edges[0], "col"), swap_even(edges[1], "col")
        rho, rho_a, rho_b = densities(state, slab_a, slab_b, col_a, col_b)
        rho_b, rho_a = swap_odd(rho_b, "col"), swap_even(rho_a, "col")
        state = moved(section == STEPS - 1, state, slab_a, slab_b, col_a, col_b, rho, rho_a, rho_b)
    return (state[0], state[1], rho[1:3])


def solution(mesh):
    placed = P(None, "slab", "col", None, None)
    return jax.shard_map(
        per_device,
        mesh=mesh,
        in_specs=(placed, placed, P("slab", "col", None)),
        out_specs=(placed, placed, P("slab", "col", None, None)),
        check_vma=False,
    )
```

```python
import functools
import math

import jax
import jax.numpy as jnp
from jax import lax
from jax.experimental import pallas as pl
from jax.experimental.pallas import tpu as pltpu
from jax.sharding import PartitionSpec as P

STEPS = 2
SLOTS = 128
MASS = 8.0 / SLOTS
KERNEL_NORM = 21.0 / (16.0 * math.pi)
TAIT = 10.0 * 10.0 / 7.0
TIME_STEP = 0.02
GRAVITY = 1.0
FAR = 1000.0
TINY = 1e-30

PARTS_J = (0, 0, 1, 1, 0, 2)
PARTS_I = (0, 1, 0, 1, 2, 0)
ROW_X = 0
ROW_NJ = 18
ROW_ONE = 21
ROW_RHO = 24
ROW_P = 27
ROW_V = 32
ROW_WJ = 50
SHORT = 32
LONG = 64
DEPTH = 128
SUM_ROWS = ((ROW_X, ROW_X + 2, ROW_X + 5), (ROW_X + 6, ROW_X + 8, ROW_X + 11), (ROW_X + 12, ROW_X + 14, ROW_X + 17))


def split3(value):
    high = value.astype(jnp.bfloat16).astype(jnp.float32)
    rest = value - high
    middle = rest.astype(jnp.bfloat16).astype(jnp.float32)
    return (high, middle, rest - middle)


def dot(lhs, rhs):
    return jnp.dot(lhs, rhs, preferred_element_type=jnp.float32)


def fold(tile):
    return jnp.sum(tile.reshape(tile.shape[0] // 8, 8, tile.shape[1]), axis=0)


def parities():
    return lax.axis_index("slab") % 2 == 0, lax.axis_index("col") % 2 == 0


def column_of(refs, comp, ix, iy):
    own, slab_a, slab_b, *cols = refs
    slab_even, col_even = parities()
    if iy in (0, 3):
        col_a, col_b = cols
        near, other = (col_b, col_a) if iy == 0 else (col_a, col_b)
        rows = lambda at: jnp.where(col_even, near[comp, at], other[comp, at])
        if 2 <= ix < 4:
            return rows(ix)
        at_a, at_b = ix % 2, 4 + ix % 2
        first, second = (at_b, at_a) if ix < 2 else (at_a, at_b)
        return jnp.where(slab_even, rows(first), rows(second))
    if 2 <= ix < 4:
        return own[comp, ix - 2, iy - 1]
    first, second = (slab_b, slab_a) if ix < 2 else (slab_a, slab_b)
    return jnp.where(slab_even, first[comp, ix % 2, iy - 1], second[comp, ix % 2, iy - 1])


def centred(refs, ix, iy):
    places = []
    for axis in range(3):
        half = 0.5 * column_of(refs, axis, ix, iy)
        if axis == 2:
            shift = lax.broadcasted_iota(jnp.int32, half.shape, 0).astype(jnp.float32) - 0.5 * half.shape[0]
        else:
            shift = (ix - 3.0, iy - 2.0)[axis]
        places.append(half + shift)
    return places


def source_rows(refs, ix, iy, with_velocity):
    live = column_of(refs, 6, ix, iy) > 0.5
    places = [jnp.where(live, place, FAR) for place in centred(refs, ix, iy)]
    rows = {}
    for axis in range(3):
        parts = split3(places[axis])
        for at, part in enumerate(PARTS_J):
            rows[ROW_X + 6 * axis + at] = parts[part]
    norm = places[0] * places[0] + places[1] * places[1] + places[2] * places[2]
    for at, part in enumerate(split3(norm)):
        rows[ROW_NJ + at] = part
        rows[ROW_ONE + at] = jnp.ones_like(part)
    if with_velocity:
        speeds = [column_of(refs, 3 + axis, ix, iy) for axis in range(3)]
        along = 0.0
        for axis in range(3):
            parts = split3(speeds[axis])
            for at, part in enumerate(PARTS_J):
                rows[ROW_V + 6 * axis + at] = parts[part]
            along = along + speeds[axis] * places[axis]
        for at, part in enumerate(split3(along)):
            rows[ROW_WJ + at] = part
    return rows


def put_rows(table, column, rows, depth):
    blank = jnp.zeros((table.shape[1], SLOTS), jnp.float32)
    for row in range(depth):
        table[column, :, row, :] = rows.get(row, blank)


def turned_cell(table, column, z):
    rows = table[column, z]
    flat = jnp.transpose(rows)
    return jnp.concatenate([flat, jnp.zeros((SLOTS, DEPTH - rows.shape[0]), jnp.float32)], axis=1).astype(jnp.bfloat16)


def deep(rows):
    return jnp.concatenate([rows, jnp.zeros((DEPTH - rows.shape[0], SLOTS), jnp.float32)], axis=0).astype(jnp.bfloat16)


def gap_rows_of(places):
    rows = {}
    for axis in range(3):
        parts = split3(-2.0 * places[axis])
        for at, part in enumerate(PARTS_I):
            rows[ROW_X + 6 * axis + at] = parts[part]
    norm = places[0] * places[0] + places[1] * places[1] + places[2] * places[2]
    for at, part in enumerate(split3(norm)):
        rows[ROW_NJ + at] = jnp.ones_like(part)
        rows[ROW_ONE + at] = part
    return rows


def closing_rows_of(places, speeds):
    rows = {}
    along = 0.0
    for axis in range(3):
        place_parts = split3(2.0 * places[axis])
        speed_parts = split3(2.0 * speeds[axis])
        for at, part in enumerate(PARTS_I):
            rows[ROW_X + 6 * axis + at] = speed_parts[part]
            rows[ROW_V + 6 * axis + at] = place_parts[part]
        along = along + places[axis] * speeds[axis]
    for at, part in enumerate(split3(-2.0 * along)):
        rows[ROW_WJ + at] = jnp.full_like(part, -2.0)
        rows[ROW_ONE + at] = part
    return rows


def sum_rows_of(value, row):
    rows = {}
    for at, part in enumerate(split3(value)):
        rows[row + at] = jnp.ones_like(part)
        rows[ROW_ONE + at] = part
    return rows


def source_ys(inner):
    return (1, 2) if inner else (0, 3)


def source_columns(inner, tx, ty):
    return [(tx + dx) * 2 + (at if inner else ty) for dx in range(3) for at in range(2 if inner else 1)]


def density_kernel(inner, refs, partial, rho_ref, table, turned, weights):
    cells_z = refs[0].shape[3]
    for ix in range(6):
        for at, iy in enumerate(source_ys(inner)):
            put_rows(table, ix * 2 + at, source_rows(refs, ix, iy, False), SHORT)

    def turn(column, carry):
        for z in range(cells_z):
            turned[column, z] = turned_cell(table, column, z)
        return carry

    lax.fori_loop(0, 12, turn, 0)
    for tx in range(4):
        for ty in range(2):
            places = centred(refs, tx + 1, ty + 1)
            put_rows(weights, tx * 2 + ty, gap_rows_of(places), SHORT)

    def target(step, carry):
        tx, ty = step // 2, step % 2
        for pair in range(cells_z // 2):
            rhs = jnp.concatenate([deep(weights[step, 2 * pair]), deep(weights[step, 2 * pair + 1])], axis=1)
            zero = jnp.zeros((8, SLOTS), jnp.float32)
            fourths, fifths = [zero, zero], [zero, zero]
            for column in source_columns(inner, tx, ty):
                for z in range(max(0, 2 * pair - 1), min(cells_z, 2 * pair + 3)):
                    gap = dot(turned[column, z], rhs)
                    for half in range(2):
                        if abs(2 * pair + half - z) > 1:
                            continue
                        near = jnp.maximum(gap[:, half * SLOTS : (half + 1) * SLOTS], TINY)
                        inside = jnp.maximum(1.0 - 1.0 / lax.rsqrt(near), 0.0)
                        square = inside * inside
                        fourth = square * square
                        fourths[half] = fourths[half] + fold(fourth)
                        fifths[half] = fifths[half] + fold(fourth * inside)
            for half in range(2):
                total = 5.0 * fourths[half] - 4.0 * fifths[half]
                row = pl.ds(2 * pair + half, 1)
                total = (MASS * KERNEL_NORM) * jnp.sum(total, axis=0, keepdims=True)
                if partial is not None:
                    total = total + partial[tx, ty, row, :]
                rho_ref[tx, ty, row, :] = total
        return carry

    lax.fori_loop(0, 8, target, 0)


def inner_density_kernel(own, slab_a, slab_b, rho_ref, *scratch):
    density_kernel(True, (own, slab_a, slab_b), None, rho_ref, *scratch)


def outer_density_kernel(own, slab_a, slab_b, col_a, col_b, partial, rho_ref, send_a, send_b, *scratch):
    density_kernel(False, (own, slab_a, slab_b, col_a, col_b), partial, rho_ref, *scratch)
    for ix in range(2):
        for iy in range(2):
            rho_ref[ix + 1, iy] = rho_ref[ix + 1, iy] + (1.0 - own[6, ix, iy]) * (MASS * KERNEL_NORM)
    col_even = parities()[1]
    for ix in range(4):
        low, high = rho_ref[ix, 0], rho_ref[ix, 1]
        send_a[ix] = jnp.where(col_even, high, low)
        send_b[ix] = jnp.where(col_even, low, high)


def pressure_ratio(density):
    cubed = density * density * density
    return TAIT * (cubed * cubed * density - 1.0) / (density * density)


def force_kernel(inner, refs, rho, rho_a, rho_b, store, table, turned, weights, long_weights, spread):
    cells_z = refs[0].shape[3]
    col_even = parities()[1]
    for ix in range(4):
        for side, iy in enumerate(source_ys(inner)):
            rows = source_rows(refs, ix + 1, iy, True)
            if iy == 0:
                density = jnp.where(col_even, rho_b[ix], rho_a[ix])
            elif iy == 3:
                density = jnp.where(col_even, rho_a[ix], rho_b[ix])
            else:
                density = rho[ix, iy - 1]
            density = jnp.maximum(density, MASS * KERNEL_NORM)
            for at, part in enumerate(split3(density)):
                rows[ROW_RHO + at] = part
            for at, part in enumerate(split3(pressure_ratio(density))):
                rows[ROW_P + at] = part
            put_rows(table, ix * 2 + side, rows, LONG)

    at_row = lax.broadcasted_iota(jnp.int32, (DEPTH, SLOTS), 0)
    picks = []
    for rows in SUM_ROWS:
        chosen = (at_row == rows[0]) | (at_row == rows[1]) | (at_row == rows[2])
        picks.append(jnp.where(chosen, 1.0, 0.0).astype(jnp.bfloat16))
    picks = jnp.concatenate(picks, axis=1)

    def turn(column, carry):
        flats = [turned_cell(table, column, z) for z in range(cells_z)]
        for z in range(cells_z):
            turned[column, z] = flats[z]
        values = dot(jnp.concatenate(flats, axis=0), picks)
        for z in range(cells_z):
            spread[column, z] = values[z * SLOTS : (z + 1) * SLOTS]
        return carry

    lax.fori_loop(0, 8, turn, 0)

    for tx in range(2):
        for ty in range(2):
            places = centred(refs, tx + 2, ty + 1)
            speeds = [column_of(refs, 3 + axis, tx + 2, ty + 1) for axis in range(3)]
            density = jnp.maximum(rho[tx + 1, ty], MASS * KERNEL_NORM)
            put_rows(weights.at[0], tx * 2 + ty, gap_rows_of(places), SHORT)
            put_rows(weights.at[1], tx * 2 + ty, sum_rows_of(density, ROW_RHO), SHORT)
            put_rows(weights.at[2], tx * 2 + ty, sum_rows_of(pressure_ratio(density), ROW_P), SHORT)
            put_rows(long_weights, tx * 2 + ty, closing_rows_of(places, speeds), LONG)

    def target(step, carry):
        tx, ty = step // 2, step % 2
        for zt in range(cells_z):
            rhs = jnp.concatenate([deep(weights[0, step, zt]), deep(long_weights[step, zt])], axis=1)
            rhs_sums = jnp.concatenate([deep(weights[1, step, zt]), deep(weights[2, step, zt])], axis=1)
            sums = [jnp.zeros((8, SLOTS), jnp.float32)] * 4
            for column in source_columns(inner, tx, ty):
                for z in range(max(0, zt - 1), min(cells_z, zt + 2)):
                    both = dot(turned[column, z], rhs)
                    pair_sums = dot(turned[column, z], rhs_sums)
                    near = jnp.maximum(both[:, :SLOTS], TINY)
                    inside = jnp.maximum(1.0 - near * lax.rsqrt(near), 0.0)
                    closing = jnp.maximum(both[:, SLOTS:], 0.0)
                    below = (near + 0.0025) * pair_sums[:, :SLOTS]
                    strength = pair_sums[:, SLOTS:] + closing / below
                    strength = strength * (inside * inside * inside)
                    for axis in range(3):
                        place = spread[column, z, :, axis * SLOTS : (axis + 1) * SLOTS]
                        sums[axis] = sums[axis] + fold(strength * place)
                    sums[3] = sums[3] + fold(strength)
            store(tx, ty, zt, [jnp.sum(total, axis=0, keepdims=True) for total in sums])
        return carry

    lax.fori_loop(0, 4, target, 0)


def inner_force_kernel(own, slab_a, slab_b, rho, sums_ref, *scratch):
    def store(tx, ty, zt, sums):
        for at in range(4):
            sums_ref[at, tx, ty, pl.ds(zt, 1), :] = sums[at]

    force_kernel(True, (own, slab_a, slab_b), rho, None, None, store, *scratch)


def outer_force_kernel(last, own, slab_a, slab_b, col_a, col_b, rho, rho_a, rho_b, partial, *outs_and_scratch):
    outs, scratch = outs_and_scratch[: 2 if last else 1], outs_and_scratch[2 if last else 1 :]

    def store(tx, ty, zt, sums):
        row = pl.ds(zt, 1)
        *parts, whole = [sums[at] + partial[at, tx, ty, row, :] for at in range(4)]
        live = own[6, tx, ty, row, :] > 0.5
        for axis in range(3):
            old_place = own[axis, tx, ty, row, :]
            old_speed = own[3 + axis, tx, ty, row, :]
            shift = zt - 0.5 * own.shape[3]
            if axis < 2:
                shift = jnp.asarray((tx, ty)[axis] - 1, jnp.int32).astype(jnp.float32)
            place = 0.5 * old_place + shift
            pull = (10.0 * KERNEL_NORM * MASS) * (place * whole - parts[axis])
            if axis == 2:
                pull = pull - GRAVITY
            speed = old_speed + TIME_STEP * pull
            new_place = jnp.where(live, old_place + TIME_STEP * speed, old_place)
            new_speed = jnp.where(live, speed, old_speed)
            if last:
                outs[0][axis, tx, ty, row, :] = new_place
                outs[1][axis, tx, ty, row, :] = new_speed
            else:
                outs[0][axis, tx, ty, row, :] = new_place
                outs[0][3 + axis, tx, ty, row, :] = new_speed
        if not last:
            outs[0][6, tx, ty, row, :] = own[6, tx, ty, row, :]

    force_kernel(False, (own, slab_a, slab_b, col_a, col_b), rho, rho_a, rho_b, store, *scratch)


VMEM_SPEC = pl.BlockSpec(memory_space=pltpu.VMEM)
INNER_WORK = 1 << 34
OUTER_WORK = 1 << 33


def shaped(*shape):
    return jax.ShapeDtypeStruct(shape, jnp.float32)


def call(kernel, name, work, outs, scratch, *operands):
    return pl.pallas_call(
        kernel,
        name=name,
        out_shape=outs,
        in_specs=[VMEM_SPEC] * len(operands),
        out_specs=jax.tree.map(lambda _: VMEM_SPEC, outs),
        scratch_shapes=scratch,
        cost_estimate=pl.CostEstimate(flops=work, bytes_accessed=1 << 19, transcendentals=0),
        compiler_params=pltpu.CompilerParams(vmem_limit_bytes=32 << 20),
    )(*operands)


def densities(inner, state, *halo):
    cells_z = state.shape[3]
    scratch = [
        pltpu.VMEM((12, cells_z, SHORT, SLOTS), jnp.float32),
        pltpu.VMEM((12, cells_z, SLOTS, DEPTH), jnp.bfloat16),
        pltpu.VMEM((8, cells_z, SHORT, SLOTS), jnp.float32),
    ]
    whole, edge = shaped(4, 2, cells_z, SLOTS), shaped(4, cells_z, SLOTS)
    if inner:
        return call(inner_density_kernel, "inner_density", INNER_WORK, whole, scratch, state, *halo)
    return call(outer_density_kernel, "outer_density", OUTER_WORK, (whole, edge, edge), scratch, state, *halo)


def forces(inner, last, state, *halo):
    cells_z = state.shape[3]
    block = state.shape[1:]
    scratch = [
        pltpu.VMEM((8, cells_z, LONG, SLOTS), jnp.float32),
        pltpu.VMEM((8, cells_z, SLOTS, DEPTH), jnp.bfloat16),
        pltpu.VMEM((3, 4, cells_z, SHORT, SLOTS), jnp.float32),
        pltpu.VMEM((4, cells_z, LONG, SLOTS), jnp.float32),
        pltpu.VMEM((8, cells_z, SLOTS, 3 * SLOTS), jnp.float32),
    ]
    if inner:
        return call(inner_force_kernel, "inner_force", INNER_WORK, shaped(4, *block), scratch, state, *halo)
    outs = (shaped(3, *block), shaped(3, *block)) if last else shaped(7, *block)
    return call(functools.partial(outer_force_kernel, last), "outer_force", OUTER_WORK, outs, scratch, state, *halo)


def swap_even(value, axis):
    return lax.ppermute(value, axis, [(i, i ^ 1) for i in range(lax.axis_size(axis))])


def swap_odd(value, axis):
    count = lax.axis_size(axis)
    return lax.ppermute(value, axis, [(i, i - 1 if i % 2 == 0 else i + 1) for i in range(1, count - 1)])


def per_device(offsets, velocity, occupancy):
    slot_rank = jnp.arange(SLOTS, dtype=jnp.int32)
    live = (slot_rank < occupancy[..., None]).astype(jnp.float32)
    state = jnp.concatenate([offsets, velocity, live[None]], axis=0)
    col_odd = lax.axis_index("col") % 2
    for section in range(STEPS):
        slab_b, slab_a = swap_odd(state, "slab"), swap_even(state, "slab")
        edges = [
            jnp.concatenate([lax.dynamic_index_in_dim(part, y, 2, keepdims=False) for part in (slab_a, state, slab_b)], axis=1)
            for y in (col_odd, 1 - col_odd)
        ]
        col_b, col_a = swap_odd(edges[0], "col"), swap_even(edges[1], "col")
        rho = densities(True, state, slab_a, slab_b)
        rho, rho_a, rho_b = densities(False, state, slab_a, slab_b, col_a, col_b, rho)
        rho_b, rho_a = swap_odd(rho_b, "col"), swap_even(rho_a, "col")
        sums = forces(True, False, state, slab_a, slab_b, rho)
        last = section == STEPS - 1
        state = forces(False, last, state, slab_a, slab_b, col_a, col_b, rho, rho_a, rho_b, sums)
    return (state[0], state[1], rho[1:3])


def solution(mesh):
    placed = P(None, "slab", "col", None, None)
    return jax.shard_map(
        per_device,
        mesh=mesh,
        in_specs=(placed, placed, P("slab", "col", None)),
        out_specs=(placed, placed, P("slab", "col", None, None)),
        check_vma=False,
    )
```
